32 devices in a mesh: clips: 2 (over y), tok: 4 (over z), head: 4 (over x, core).
Axes of the slice: x: 2, y: 2, z: 4, core: 2. Of those that a mesh axis runs over, the one named last changes fastest.
Arguments:
- query: bfloat16 [24, 256, 1536], P(('clips', 'tok'), 'head'), parts along dimension 0, may hold values from -16 to 16, as said below
- key: bfloat16 [24, 256, 1536], P(('clips', 'tok'), 'head'), parts along dimension 0, may hold values from -16 to 16
- value: bfloat16 [24, 256, 1536], P(('clips', 'tok'), 'head'), parts along dimension 0, may hold values from -6 to 6
- valid_rows: int32 [24], P(('clips', 'tok')), parts along dimension 0, may hold values from 1 to 8, as said below
Outputs:
- attended: bfloat16 [24, 256, 1536], P(('clips', 'tok'), 'head'), parts along dimension 0
The draws below stay inside these ranges and needn't reach their ends.
There are 2 independent parts, one for each index of `clips`. The reference program is written for one: setup_inputs(seed, part) draws one part's arguments, and reference() takes and returns one part's arrays. A program takes and returns all parts, laid end to end along the dimension named above; each array names one. Nothing has to cross between parts.
Inputs may be any that keep to these rules, and one draw needn't show every extreme that they name: Entries of query and key lie within -16 and 16. `valid_rows`: tiles outside the last height-tile row have all 8 rows real; tiles of the last height-tile row each have their own count.
All inputs are finite; a program needn't handle non-finite values.
Results may differ from the reference program's by a relative error of at most 0.0031.
Values may be sent and summed in bfloat16 or wider, within the bound.
A program may use at most 64 MiB of HBM per device.

```python
import math
import jax
import jax.numpy as jnp
from jax import lax

HEADS = 12
HEAD_DIM = 128
TILE_H = 8
TILE_W = 8
TIME_TILES = 4
WIDTH_TILES = 3
HEIGHT_TILES = 1
TILE = 256
TILES = 12


def pair_fields(key):
    shape = (TILES, TILE, HEADS * HEAD_DIM)
    base_q = 1.6 * jnp.clip(jax.random.normal(jax.random.fold_in(key, 11), shape, jnp.float32), -4.0, 4.0)
    base_k = 1.6 * jnp.clip(jax.random.normal(jax.random.fold_in(key, 12), shape, jnp.float32), -4.0, 4.0)
    return (base_q, base_k)


def draw_query(key, part):
    return pair_fields(key)[0].astype(jnp.bfloat16)


def draw_key(key, part):
    return pair_fields(key)[1].astype(jnp.bfloat16)


def draw_valid_rows(key, part):
    tile_id = jnp.arange(TILES)
    random_counts = jax.random.randint(jax.random.fold_in(key, 21), (TILES,), 1, TILE_H + 1)
    height_pos = tile_id // WIDTH_TILES % HEIGHT_TILES
    time_pos = tile_id // (WIDTH_TILES * HEIGHT_TILES)
    bottom = height_pos == HEIGHT_TILES - 1
    bottom_counts = jnp.where(time_pos == 1, TILE_H, jnp.where(time_pos == 2, 1, random_counts))
    rows = jnp.where(bottom, bottom_counts, TILE_H)
    return rows.astype(jnp.int32)


def block_scale(rng, shape, pieces, low, high):
    gain, own = 1.0, jax.random.fold_in(rng, 6)
    for dim, blocks in pieces:
        steps = jnp.exp(jax.random.uniform(jax.random.fold_in(own, dim), (blocks,), jnp.float32, low / len(pieces), high / len(pieces)))
        gain = gain * jnp.repeat(steps, shape[dim] // blocks).reshape([-1 if axis == dim else 1 for axis in range(len(shape))])
    return gain


def scatter_about(stream_key, shape, deviation, bound, pieces=(), kind=jnp.bfloat16):
    array = jax.random.normal(stream_key, shape, jnp.float32) * deviation
    if len(pieces) > 0:
        array = block_scale(stream_key, shape, pieces, -0.22, 0.18) * array
    return jnp.clip(array, min=-bound, max=bound).astype(kind)


def setup_inputs(seed: int = 0, part: int = 0) -> dict:
    key_list = jax.random.split(jax.random.key(seed), 5)
    part_splits = jax.random.split(jax.random.fold_in(key_list[4], part), 5)
    query = draw_query(jax.random.fold_in(jax.random.fold_in(key_list[4], part), 71), part)
    key = draw_key(jax.random.fold_in(jax.random.fold_in(key_list[4], part), 71), part)
    value = scatter_about(part_splits[2], (TILES, TILE, HEADS * HEAD_DIM), 1.0, 6.0, ((0, 4), (1, 4)))
    valid_rows = draw_valid_rows(jax.random.fold_in(jax.random.fold_in(key_list[4], part), 71), part)
    return {"query": query, "key": key, "value": value, "valid_rows": valid_rows}


def reference(query, key, value, valid_rows):
    grid = (TIME_TILES, HEIGHT_TILES, WIDTH_TILES)
    scale = 1.0 / math.sqrt(HEAD_DIM)

    def per_head(field):
        return jnp.moveaxis(field.reshape(grid + (TILE, HEADS, HEAD_DIM)), 4, 0)
    counts = jnp.pad(valid_rows.reshape(grid), 1)
    count_win = jnp.stack([counts[a:a + TIME_TILES, b:b + HEIGHT_TILES, c:c + WIDTH_TILES] for a in range(3) for b in range(3) for c in range(3)], axis=-1)
    row_index = jnp.arange(TILE) // TILE_W % TILE_H
    mask = (row_index[None, None, None, None, :] < count_win[..., None]).reshape(grid + (27 * TILE,))

    def window(field):
        padded = jnp.pad(field, ((1, 1), (1, 1), (1, 1), (0, 0), (0, 0)))
        parts = [padded[a:a + TIME_TILES, b:b + HEIGHT_TILES, c:c + WIDTH_TILES] for a in range(3) for b in range(3) for c in range(3)]
        return jnp.stack(parts, axis=3).reshape(grid + (27 * TILE, HEAD_DIM))

    def one_head(items):
        q_head, k_head, v_head = items
        k_win = window(k_head)
        v_win = window(v_head)

        def one_time(inner):
            q_part, k_part, v_part, m_part = inner
            scores = jnp.einsum('bcqd,bckd->bcqk', q_part.astype(jnp.float32), k_part.astype(jnp.float32)) * scale
            scores = jnp.where(m_part[:, :, None, :], scores, -jnp.inf)
            largest = lax.optimization_barrier(jnp.max(scores, axis=-1, keepdims=True))
            weight = jnp.exp(scores - largest)
            total = lax.optimization_barrier(jnp.sum(weight, axis=-1, keepdims=True))
            rounded = weight.astype(jnp.bfloat16)
            summed = jnp.einsum('bcqk,bckd->bcqd', rounded.astype(jnp.float32), v_part.astype(jnp.float32))
            return (summed / total).astype(jnp.bfloat16)
        return lax.map(one_time, (q_head, k_win, v_win, mask))
    result = lax.map(one_head, (per_head(query), per_head(key), per_head(value)))
    result = jnp.moveaxis(result, 0, 4)
    return result.reshape(TILES, TILE, HEADS * HEAD_DIM)
```

```python
import functools
import math

import jax
import jax.numpy as jnp
from jax import lax
from jax.experimental import pallas as pl
from jax.experimental.pallas import tpu as pltpu
from jax.sharding import PartitionSpec as P

HEAD_DIM = 128
TILE_H = 8
TILE_W = 8
TIME_TILES = 4
MESH = pl.DeviceIdType.MESH
GAIN = math.log2(math.e) / math.sqrt(HEAD_DIM)


def window_slots(rows_grid):
    sides = (-1, 0, 1) if rows_grid > 1 else (0,)
    around = [(down, side) for down in (-1, 0, 1) for side in sides if (down, side) != (0, 0)]
    return [(0, 0)] + around


def kernel(
    heads_axis, rows_grid,
    q_hbm, k_hbm, v_hbm, count_hbm, out_hbm,
    q_buf, k_buf, v_buf, bias_buf, s_buf, p_buf, inv_buf, acc_buf, o_buf, rows_buf, count_buf,
    local_sem, qx_send, qx_recv, kx_send, kx_recv, vx_send, vx_recv,
    bz_send, bz_recv, kz_send, kz_recv, vz_send, vz_recv, ox_send, ox_recv,
):
    slots = window_slots(rows_grid)
    width, part = q_hbm.shape[0], q_hbm.shape[1]
    tile_len, feats = q_buf.shape[1], q_buf.shape[2]
    local = feats // HEAD_DIM
    me = lax.axis_index("head")
    tok = lax.axis_index("tok")
    time, height = tok // rows_grid, tok % rows_grid
    steps = range(1, heads_axis)
    far_first = list(reversed(steps))

    def exists(j):
        down, side = slots[j]
        ok = (time + down >= 0) & (time + down < TIME_TILES)
        if side != 0:
            ok = ok & (height + side >= 0) & (height + side < rows_grid)
        return ok

    def around(j):
        return tok + slots[j][0] * rows_grid + slots[j][1]

    def opposite(j):
        return slots.index((-slots[j][0], -slots[j][1]))

    def peer(s):
        return me ^ s

    def rows(g):
        return pl.ds(pl.multiple_of(g * part, part), part)

    def cols(g):
        return pl.ds(pl.multiple_of(g * feats, feats), feats)

    def head_cols(h):
        return pl.ds(pl.multiple_of(h * HEAD_DIM, HEAD_DIM), HEAD_DIM)

    def global_cols(g, h):
        return pl.ds(pl.multiple_of((g * local + h) * HEAD_DIM, HEAD_DIM), HEAD_DIM)

    def remote(src, dst, send, recv, device):
        return pltpu.make_async_remote_copy(
            src_ref=src, dst_ref=dst, send_sem=send, recv_sem=recv,
            device_id=device, device_id_type=MESH,
        )

    def qx(s, owner):
        return remote(q_hbm.at[:, :, cols(peer(s))], q_buf.at[:, rows(owner), :],
                      qx_send.at[s], qx_recv.at[s], {"head": peer(s)})

    def kx(s, owner):
        return remote(k_hbm.at[:, :, cols(peer(s))], k_buf.at[0, :, rows(owner), :],
                      kx_send.at[s], kx_recv.at[s], {"head": peer(s)})

    def vx(h, n, s, owner):
        return remote(v_hbm.at[n, :, global_cols(peer(s), h)],
                      v_buf.at[0, n, rows(owner), head_cols(h)],
                      vx_send.at[h, n, s], vx_recv.at[h, n, s], {"head": peer(s)})

    def kz(j, s, slot):
        src = k_hbm.at[:, :, cols(me)] if s == 0 else k_buf.at[0, :, rows(peer(s)), :]
        return remote(src, k_buf.at[slot, :, rows(peer(s)), :],
                      kz_send.at[j, s], kz_recv.at[slot, s], {"tok": around(j)})

    def vz(j, h, n, s, slot):
        src = v_hbm.at[n, :, global_cols(me, h)] if s == 0 else v_buf.at[0, n, rows(peer(s)), head_cols(h)]
        return remote(src, v_buf.at[slot, n, rows(peer(s)), head_cols(h)],
                      vz_send.at[j, h, n, s], vz_recv.at[slot, h, n, s], {"tok": around(j)})

    def bz(j, slot):
        return remote(rows_buf.at[0], rows_buf.at[slot], bz_send.at[j], bz_recv.at[slot], {"tok": around(j)})

    def ox(h, c, s, owner):
        return remote(o_buf.at[c, rows(peer(s)), head_cols(h)],
                      out_hbm.at[c, :, global_cols(owner, h)],
                      ox_send.at[h, c, s], ox_recv.at[h, c, s], {"head": peer(s)})

    def each_neighbour(act):
        for j in range(1, len(slots)):
            pl.when(exists(j))(functools.partial(act, j))

    local_q = pltpu.make_async_copy(q_hbm.at[:, :, cols(me)], q_buf.at[:, rows(me), :], local_sem.at[0])
    local_k = pltpu.make_async_copy(k_hbm.at[:, :, cols(me)], k_buf.at[0, :, rows(me), :], local_sem.at[1])
    local_v = pltpu.make_async_copy(v_hbm.at[:, :, cols(me)], v_buf.at[0, :, rows(me), :], local_sem.at[2])
    local_c = pltpu.make_async_copy(count_hbm, count_buf, local_sem.at[3])

    barrier = pltpu.get_barrier_semaphore()
    for s in steps:
        pl.semaphore_signal(barrier, inc=1, device_id={"head": peer(s)}, device_id_type=MESH)
    partners = heads_axis - 1

    def greet(j):
        pl.semaphore_signal(barrier, inc=1, device_id={"tok": around(j)}, device_id_type=MESH)

    each_neighbour(greet)
    for j in range(1, len(slots)):
        partners = partners + jnp.where(exists(j), 1, 0)
    for copy in (local_c, local_q, local_k, local_v):
        copy.start()
    pl.semaphore_wait(barrier, partners)

    for s in far_first:
        kx(s, me).start()
    each_neighbour(lambda j: kz(j, 0, opposite(j)).start())
    for s in far_first:
        qx(s, me).start()
    for h in range(local):
        for n in range(width):
            for s in far_first:
                vx(h, n, s, me).start()

    local_c.wait()
    line = lax.broadcasted_iota(jnp.int32, rows_buf.shape[1:], 0)
    counts = jnp.zeros(rows_buf.shape[1:], jnp.int32)
    for n in range(width):
        counts = jnp.where(line == n, count_buf[n], counts)
    rows_buf[0] = counts

    for j in range(1, len(slots)):
        @pl.when(jnp.logical_not(exists(j)))
        def _(j=j):
            k_buf[j] = jnp.zeros(k_buf.shape[1:], k_buf.dtype)
            v_buf[j] = jnp.zeros(v_buf.shape[1:], v_buf.dtype)
            rows_buf[j] = jnp.zeros(rows_buf.shape[1:], rows_buf.dtype)

    order = [1] + [s for s in far_first if s != 1] if heads_axis > 1 else []
    for s in order:
        kx(s, peer(s)).wait_recv()
        each_neighbour(lambda j, s=s: kz(j, s, opposite(j)).start())
    near = [s for s in steps if s == 1]
    later = [s for s in order if s != 1]
    each_neighbour(lambda j: bz(j, opposite(j)).start())

    def values_on(h, n, s):
        if s != 0:
            vx(h, n, s, peer(s)).wait_recv()
        each_neighbour(lambda j: vz(j, h, n, s, opposite(j)).start())

    for h in range(local):
        for n in range(width):
            for s in [0] + near:
                values_on(h, n, s)

    for copy in (local_q, local_k, local_v):
        copy.wait()
    for s in steps:
        qx(s, peer(s)).wait_recv()

    def keys_in(j):
        bz(j, j).wait_recv()
        for s in range(heads_axis):
            kz(j, s, j).wait_recv()

    each_neighbour(keys_in)

    row = lax.broadcasted_iota(jnp.int32, bias_buf.shape[2:], 1) // TILE_W % TILE_H
    for j in range(len(slots)):
        for n in range(width):
            real = jnp.broadcast_to(rows_buf[j, n:n + 1, 0:1], row.shape)
            bias_buf[j, n] = jnp.where(row < real, 0.0, -jnp.inf)

    def window(c):
        return [(j, n) for j in range(len(slots)) for n in range(width) if abs(n - c) <= 1]

    def weigh(h, carry):
        for c in range(width):
            scratch = s_buf.at[c % s_buf.shape[0]]
            q = q_buf[c, :, head_cols(h)]
            top = None
            for i, (j, n) in enumerate(window(c)):
                s = lax.dot_general(q, k_buf[j, n, :, head_cols(h)], (((1,), (1,)), ((), ())),
                                    preferred_element_type=jnp.float32)
                s = s + bias_buf[j, n, 0:1, :]
                scratch[:, i * tile_len:(i + 1) * tile_len] = s
                for half in range(0, tile_len, 128):
                    piece = s[:, half:half + 128]
                    top = piece if top is None else jnp.maximum(top, piece)
            largest = jnp.max(top, axis=-1, keepdims=True)
            total = None
            for i in range(len(window(c))):
                for half in range(0, tile_len, 128):
                    at = slice(i * tile_len + half, i * tile_len + half + 128)
                    weight = jnp.exp2((scratch[:, at] - largest) * GAIN)
                    total = weight if total is None else total + weight
                    p_buf[h, c, :, at] = weight.astype(jnp.bfloat16)
            inverse = 1.0 / jnp.sum(total, axis=-1, keepdims=True)
            inv_buf[h, c] = jnp.broadcast_to(inverse, (tile_len, HEAD_DIM))
        for n in range(width):
            for s in later:
                values_on(h, n, s)
        return carry

    lax.fori_loop(0, local, weigh, 0)

    def local_out(h, c):
        return pltpu.make_async_copy(o_buf.at[c, rows(me), head_cols(h)],
                                     out_hbm.at[c, :, global_cols(me, h)], local_sem.at[4 + h * width + c])

    if heads_axis % 2 == 0:
        half = heads_axis // 2
        span = tile_len // 2
        side = me // half
        blocks = [
            (pl.ds(pl.multiple_of((1 - side) * span, span), span), [s for s in far_first if s >= half]),
            (pl.ds(pl.multiple_of(side * span, span), span), [s for s in far_first if s < half]),
        ]
    else:
        blocks = [(slice(None), far_first)]

    def mix(h, carry):
        def gather(c, at, picked):
            summed = None
            for i, (j, n) in enumerate(window(c)):
                if picked(j, n):
                    term = jnp.dot(p_buf[h, c, at, i * tile_len:(i + 1) * tile_len],
                                   v_buf[j, n, :, head_cols(h)], preferred_element_type=jnp.float32)
                    summed = term if summed is None else summed + term
            return summed

        for c in range(width):
            acc_buf[c] = gather(c, slice(None), lambda j, n: j == 0)
        for n in range(width):
            def values_in(j, n=n):
                for s in range(heads_axis):
                    vz(j, h, n, s, j).wait_recv()

            each_neighbour(values_in)
            here = [c for c in range(width) if abs(n - c) <= 1]
            done = [c for c in here if n == min(c + 1, width - 1)]
            for at, partners_at in blocks:
                for c in done:
                    summed = acc_buf[c, at] + gather(c, at, lambda j, m: j != 0 and m == n)
                    o_buf[c, at, head_cols(h)] = (summed * inv_buf[h, c, at]).astype(o_buf.dtype)
                    for s in partners_at:
                        ox(h, c, s, me).start()
            for c in done:
                local_out(h, c).start()
            for c in here:
                if c not in done:
                    acc_buf[c] = acc_buf[c] + gather(c, slice(None), lambda j, m: j != 0 and m == n)
        return carry

    lax.fori_loop(0, local, mix, 0)

    for s in steps:
        kx(s, me).wait_send()
        qx(s, me).wait_send()
        for h in range(local):
            for n in range(width):
                vx(h, n, s, me).wait_send()

    def sent(j):
        bz(j, opposite(j)).wait_send()
        for s in range(heads_axis):
            kz(j, s, opposite(j)).wait_send()
            for h in range(local):
                for n in range(width):
                    vz(j, h, n, s, opposite(j)).wait_send()

    each_neighbour(sent)
    for h in range(local):
        for c in range(width):
            local_out(h, c).wait()
            for s in steps:
                ox(h, c, s, me).wait_send()
                ox(h, c, s, peer(s)).wait_recv()


def body(heads_axis, tok_axis, query, key, value, valid_rows):
    width, part, wide = query.shape
    rows_grid = tok_axis // TIME_TILES
    tile_len, feats = part * heads_axis, wide // heads_axis
    local = feats // HEAD_DIM
    slots = len(window_slots(rows_grid))
    most = slots * min(width, 3) * tile_len
    dma = pltpu.SemaphoreType.DMA
    any_space = pl.BlockSpec(memory_space=pl.ANY)
    return pl.pallas_call(
        functools.partial(kernel, heads_axis, rows_grid),
        out_shape=jax.ShapeDtypeStruct(query.shape, query.dtype),
        in_specs=[pl.BlockSpec(memory_space=pltpu.HBM)] * 4,
        out_specs=any_space,
        scratch_shapes=[
            pltpu.VMEM((width, tile_len, feats), jnp.bfloat16),
            pltpu.VMEM((slots, width, tile_len, feats), jnp.bfloat16),
            pltpu.VMEM((slots, width, tile_len, feats), jnp.bfloat16),
            pltpu.VMEM((slots, width, 8, tile_len), jnp.float32),
            pltpu.VMEM((3 if slots <= 3 else 1, tile_len, most), jnp.float32),
            pltpu.VMEM((local, width, tile_len, most), jnp.bfloat16),
            pltpu.VMEM((local, width, tile_len, HEAD_DIM), jnp.float32),
            pltpu.VMEM((width, tile_len, HEAD_DIM), jnp.float32),
            pltpu.VMEM((width, tile_len, feats), jnp.bfloat16),
            pltpu.VMEM((slots, -(-width // 8) * 8, 128), jnp.int32),
            pltpu.SMEM((width,), jnp.int32),
            dma((4 + local * width,)),
            dma((heads_axis,)), dma((heads_axis,)),
            dma((heads_axis,)), dma((heads_axis,)),
            dma((local, width, heads_axis)), dma((local, width, heads_axis)),
            dma((slots,)), dma((slots,)),
            dma((slots, heads_axis)), dma((slots, heads_axis)),
            dma((slots, local, width, heads_axis)), dma((slots, local, width, heads_axis)),
            dma((local, width, heads_axis)), dma((local, width, heads_axis)),
        ],
        compiler_params=pltpu.CompilerParams(
            collective_id=0, has_side_effects=True, vmem_limit_bytes=36_000_000 if slots <= 3 else 63_000_000
        ),
    )(*(pltpu.with_memory_space_constraint(x, pltpu.HBM) for x in (query, key, value, valid_rows)))


def by_head(
    q_hbm, k_hbm, v_hbm, count_hbm, out_hbm,
    q_buf, k_buf, v_buf, bias_buf, s_buf, p_buf, inv_buf, acc_buf, o_buf, rows_buf, count_buf,
    lq_sem, lk_sem, lv_sem, lc_sem, lo_sem, qx_send, qx_recv, kx_send, kx_recv, vx_send, vx_recv,
    bz_send, bz_recv, kz_send, kz_recv, vz_send, vz_recv, ox_send, ox_recv,
):
    local, width, tile_len = q_buf.shape[0], q_buf.shape[1], q_buf.shape[2]
    part = q_hbm.shape[1]
    me = lax.axis_index("head")
    tok = lax.axis_index("tok")
    side = me // 2
    half = tile_len // 2
    far, last = (3, 2), local - 1
    slots = (0, -1, 1)
    opposite = (0, 2, 1)

    def exists(j):
        return (tok + slots[j] >= 0) & (tok + slots[j] < TIME_TILES)

    def peer(s):
        return me ^ s

    def rows(g):
        return pl.ds(pl.multiple_of(g * part, part), part)

    def cols(g, h):
        return pl.ds(pl.multiple_of((g * local + h) * HEAD_DIM, HEAD_DIM), HEAD_DIM)

    def remote(src, dst, send, recv, device):
        return pltpu.make_async_remote_copy(
            src_ref=src, dst_ref=dst, send_sem=send, recv_sem=recv,
            device_id=device, device_id_type=MESH,
        )

    def spread(hbm, buf, send, recv):
        def copy(h, s, owner):
            return remote(hbm.at[:, :, cols(peer(s), h)], buf(h).at[:, rows(owner), :],
                          send.at[h, s], recv.at[h, s], {"head": peer(s)})
        return copy

    qx = spread(q_hbm, lambda h: q_buf.at[h], qx_send, qx_recv)
    kx = spread(k_hbm, lambda h: k_buf.at[0, h], kx_send, kx_recv)
    vx = spread(v_hbm, lambda h: v_buf.at[0, h], vx_send, vx_recv)

    def along(buf, send, recv):
        def copy(j, h, s, slot, n=None):
            pick = slice(None) if n is None else slice(n, n + 1)
            at = 0 if n is None else n
            return remote(buf.at[0, h, pick, rows(peer(s)), :], buf.at[slot, h, pick, rows(peer(s)), :],
                          send.at[j, h, s, at], recv.at[slot, h, s, at], {"tok": tok + slots[j]})
        return copy

    kz = along(k_buf, kz_send, kz_recv)
    vz = along(v_buf, vz_send, vz_recv)

    def vz_tiles(h, s):
        return tuple(range(width)) if h == last and s in far else (None,)

    def bz(j, slot):
        return remote(rows_buf.at[0], rows_buf.at[slot], bz_send.at[j], bz_recv.at[slot], {"tok": tok + slots[j]})

    def ox(h, c, s, owner):
        return remote(o_buf.at[h, c, rows(peer(s)), :], out_hbm.at[c, :, cols(owner, h)],
                      ox_send.at[h, c, s], ox_recv.at[h, c, s], {"head": peer(s)})

    def own(hbm, buf, sem):
        return [pltpu.make_async_copy(hbm.at[:, :, cols(me, h)], buf(h).at[:, rows(me), :], sem.at[h])
                for h in range(local)]

    own_k = own(k_hbm, lambda h: k_buf.at[0, h], lk_sem)
    own_v = own(v_hbm, lambda h: v_buf.at[0, h], lv_sem)
    own_q = own(q_hbm, lambda h: q_buf.at[h], lq_sem)
    own_c = pltpu.make_async_copy(count_hbm, count_buf, lc_sem)

    def own_o(h, c):
        return pltpu.make_async_copy(o_buf.at[h, c, rows(me), :], out_hbm.at[c, :, cols(me, h)], lo_sem.at[h, c])

    def each_neighbour(act):
        for j in (1, 2):
            pl.when(exists(j))(functools.partial(act, j))

    barrier = pltpu.get_barrier_semaphore()

    def greet(j):
        pl.semaphore_signal(barrier, inc=1, device_id={"tok": tok + slots[j]}, device_id_type=MESH)

    each_neighbour(greet)
    for s in (2, 3, 1):
        pl.semaphore_signal(barrier, inc=1, device_id={"head": peer(s)}, device_id_type=MESH)
    own_c.start()
    for h in range(local):
        own_k[h].start()
        own_v[h].start()
    for h in range(local):
        own_q[h].start()
    for j in (1, 2):
        @pl.when(jnp.logical_not(exists(j)))
        def _(j=j):
            k_buf[j] = jnp.zeros(k_buf.shape[1:], k_buf.dtype)
            v_buf[j] = jnp.zeros(v_buf.shape[1:], v_buf.dtype)
            rows_buf[j] = jnp.zeros(rows_buf.shape[1:], rows_buf.dtype)
    own_c.wait()
    line = lax.broadcasted_iota(jnp.int32, rows_buf.shape[1:], 0)
    counts = jnp.zeros(rows_buf.shape[1:], jnp.int32)
    for n in range(width):
        counts = jnp.where(line == n, count_buf[n], counts)
    rows_buf[0] = counts
    for h in range(local):
        own_k[h].wait()
        own_v[h].wait()
    pl.semaphore_wait(barrier, 3 + jnp.where(exists(1), 1, 0) + jnp.where(exists(2), 1, 0))

    def across(copy, h):
        for s in far:
            copy(h, s, me).start()

    def beside(copy, h):
        copy(h, 1, me).start()

    def onward(copy, h, s, tiles=(None,)):
        def act(j):
            for n in tiles:
                copy(j, h, s, opposite[j], n).start()
        each_neighbour(act)

    def onward_v(h, s):
        onward(vz, h, s, vz_tiles(h, s))

    across(kx, 0)
    onward(kz, 0, 0)
    beside(kx, 0)
    across(vx, 0)
    onward_v(0, 0)
    beside(vx, 0)
    across(qx, 0)
    for h in range(1, local):
        beside(kx, h)
        beside(vx, h)
    across(kx, 1)
    onward(kz, 1, 0)
    across(vx, 1)
    onward_v(1, 0)
    across(kx, 2)
    across(qx, 1)
    across(vx, 2)
    across(qx, 2)
    each_neighbour(lambda j: bz(j, opposite[j]).start())
    for h in range(local):
        beside(qx, h)

    for h in (0, 1):
        kx(h, 1, peer(1)).wait_recv()
        onward(kz, h, 1)
        vx(h, 1, peer(1)).wait_recv()
        onward_v(h, 1)
    for s in far:
        kx(0, s, peer(s)).wait_recv()
        onward(kz, 0, s)
    for s in far:
        vx(0, s, peer(s)).wait_recv()
        onward_v(0, s)
    onward(kz, last, 0)
    kx(last, 1, peer(1)).wait_recv()
    onward(kz, last, 1)
    vx(last, 1, peer(1)).wait_recv()

    each_neighbour(lambda j: bz(j, j).wait_recv())
    row = lax.broadcasted_iota(jnp.int32, bias_buf.shape[2:], 1) // TILE_W % TILE_H
    for j in range(3):
        for n in range(width):
            real = jnp.broadcast_to(rows_buf[j, n:n + 1, 0:1], row.shape)
            bias_buf[j, n] = jnp.where(row < real, 0.0, -jnp.inf)

    for s in far:
        kx(1, s, peer(s)).wait_recv()
        onward(kz, 1, s)
    for s in far:
        vx(1, s, peer(s)).wait_recv()
        onward_v(1, s)

    def window(c):
        return [(j, n) for j in range(3) for n in range(width) if abs(n - c) <= 1]

    def queries_in(h):
        own_q[h].wait()
        for s in (1, 2, 3):
            qx(h, s, peer(s)).wait_recv()

    def keys_in(h):
        def act(j):
            for s in range(4):
                kz(j, h, s, j).wait_recv()
        each_neighbour(act)

    def values_in(h, which, tiles=None):
        def act(j):
            for s in which:
                for n in (tiles if tiles is not None else vz_tiles(h, s)):
                    vz(j, h, s, j, n).wait_recv()
        each_neighbour(act)

    def weigh(h):
        for c in range(width):
            scratch = s_buf.at[c]
            q = q_buf[h, c]
            top = None
            for i, (j, n) in enumerate(window(c)):
                s = lax.dot_general(q, k_buf[j, h, n], (((1,), (1,)), ((), ())),
                                    preferred_element_type=jnp.float32)
                s = s + bias_buf[j, n, 0:1, :]
                scratch[:, i * tile_len:(i + 1) * tile_len] = s
                for at in range(0, tile_len, 128):
                    piece = s[:, at:at + 128]
                    top = piece if top is None else jnp.maximum(top, piece)
            largest = jnp.max(top, axis=-1, keepdims=True)
            total = None
            for i in range(len(window(c))):
                for at in range(0, tile_len, 128):
                    at = slice(i * tile_len + at, i * tile_len + at + 128)
                    weight = jnp.exp2((scratch[:, at] - largest) * GAIN)
                    total = weight if total is None else total + weight
                    p_buf[c, :, at] = weight.astype(jnp.bfloat16)
            inverse = 1.0 / jnp.sum(total, axis=-1, keepdims=True)
            inv_buf[c] = jnp.broadcast_to(inverse, (tile_len, HEAD_DIM))

    there = pl.ds(pl.multiple_of((1 - side) * half, half), half)
    here = pl.ds(pl.multiple_of(side * half, half), half)
    blocks = ((there, far), (here, (1,)))

    def mixed(h, c, at, picked, keys=None):
        summed = None
        for i, (j, n) in enumerate(window(c)):
            if picked(j, n):
                if keys is None:
                    p, v = p_buf[c, at, i * tile_len:(i + 1) * tile_len], v_buf[j, h, n]
                else:
                    span = pl.ds(pl.multiple_of(i * tile_len + keys * half, half), half)
                    p, v = p_buf[c, at, span], v_buf[j, h, n, pl.ds(pl.multiple_of(keys * half, half), half), :]
                term = jnp.dot(p, v, preferred_element_type=jnp.float32)
                summed = term if summed is None else summed + term
        return summed

    def leave(h, c, at, partners, summed):
        o_buf[h, c, at, :] = (summed * inv_buf[c, at]).astype(o_buf.dtype)
        for s in partners:
            ox(h, c, s, me).start()

    def mix(h):
        for c in range(width):
            for at, partners in blocks:
                leave(h, c, at, partners, mixed(h, c, at, lambda j, n: True))
            own_o(h, c).start()

    def mix_last(h):
        for c in range(width):
            acc_buf[c] = mixed(h, c, slice(None), lambda j, n: j == 0)
        values_in(h, (0, 1))
        for c in range(width):
            acc_buf[c] = acc_buf[c] + mixed(h, c, slice(None), lambda j, n: j != 0, side)
        for n in range(width):
            values_in(h, far, (n,))
            near = [c for c in range(width) if abs(n - c) <= 1]
            done = [c for c in near if n == min(c + 1, width - 1)]
            for at, partners in blocks:
                for c in done:
                    leave(h, c, at, partners,
                          acc_buf[c, at] + mixed(h, c, at, lambda j, m: j != 0 and m == n, 1 - side))
            for c in done:
                own_o(h, c).start()
            for c in near:
                if c not in done:
                    acc_buf[c] = acc_buf[c] + mixed(h, c, slice(None), lambda j, m: j != 0 and m == n, 1 - side)

    queries_in(0)
    keys_in(0)
    weigh(0)
    for s in far:
        kx(last, s, peer(s)).wait_recv()
        onward(kz, last, s)
    onward_v(last, 0)
    onward_v(last, 1)
    values_in(0, range(4))
    mix(0)
    for s in far:
        vx(last, s, peer(s)).wait_recv()
    for n in range(width):
        for s in far:
            onward(vz, last, s, (n,))
    queries_in(1)
    keys_in(1)
    weigh(1)
    values_in(1, range(4))
    mix(1)
    queries_in(last)
    keys_in(last)
    weigh(last)
    mix_last(last)

    for h in range(local):
        for s in (1, 2, 3):
            kx(h, s, me).wait_send()
            vx(h, s, me).wait_send()
            qx(h, s, me).wait_send()

    def sent(j):
        bz(j, opposite[j]).wait_send()
        for h in range(local):
            for s in range(4):
                kz(j, h, s, opposite[j]).wait_send()
                for n in vz_tiles(h, s):
                    vz(j, h, s, opposite[j], n).wait_send()

    each_neighbour(sent)
    for h in range(local):
        for c in range(width):
            own_o(h, c).wait()
            for s in (1, 2, 3):
                ox(h, c, s, me).wait_send()
                ox(h, c, s, peer(s)).wait_recv()


def body_by_head(query, key, value, valid_rows):
    width, part, wide = query.shape
    tile_len, local = part * 4, wide // 4 // HEAD_DIM
    most = 3 * min(width, 3) * tile_len
    dma = pltpu.SemaphoreType.DMA
    return pl.pallas_call(
        by_head,
        out_shape=jax.ShapeDtypeStruct(query.shape, query.dtype),
        in_specs=[pl.BlockSpec(memory_space=pltpu.HBM)] * 4,
        out_specs=pl.BlockSpec(memory_space=pl.ANY),
        scratch_shapes=[
            pltpu.VMEM((local, width, tile_len, HEAD_DIM), jnp.bfloat16),
            pltpu.VMEM((3, local, width, tile_len, HEAD_DIM), jnp.bfloat16),
            pltpu.VMEM((3, local, width, tile_len, HEAD_DIM), jnp.bfloat16),
            pltpu.VMEM((3, width, 8, tile_len), jnp.float32),
            pltpu.VMEM((width, tile_len, most), jnp.float32),
            pltpu.VMEM((width, tile_len, most), jnp.bfloat16),
            pltpu.VMEM((width, tile_len, HEAD_DIM), jnp.float32),
            pltpu.VMEM((width, tile_len, HEAD_DIM), jnp.float32),
            pltpu.VMEM((local, width, tile_len, HEAD_DIM), jnp.bfloat16),
            pltpu.VMEM((3, -(-width // 8) * 8, 128), jnp.int32),
            pltpu.SMEM((width,), jnp.int32),
            dma((local,)), dma((local,)), dma((local,)), dma(()), dma((local, width)),
            dma((local, 4)), dma((local, 4)), dma((local, 4)), dma((local, 4)), dma((local, 4)), dma((local, 4)),
            dma((3,)), dma((3,)),
            dma((3, local, 4, 1)), dma((3, local, 4, 1)),
            dma((3, local, 4, width)), dma((3, local, 4, width)),
            dma((local, width, 4)), dma((local, width, 4)),
        ],
        compiler_params=pltpu.CompilerParams(
            collective_id=0, has_side_effects=True, vmem_limit_bytes=36_000_000
        ),
    )(*(pltpu.with_memory_space_constraint(x, pltpu.HBM) for x in (query, key, value, valid_rows)))


def solution(mesh):
    placed = (
        P(("clips", "tok"), "head", None),
        P(("clips", "tok"), "head", None),
        P(("clips", "tok"), "head", None),
        P(("clips", "tok")),
    )
    heads_axis, tok_axis = mesh.shape["head"], mesh.shape["tok"]

    def step(query, key, value, valid_rows):
        if heads_axis == 4 and tok_axis == TIME_TILES and query.shape[2] == 4 * 3 * HEAD_DIM:
            return body_by_head(query, key, value, valid_rows)
        return body(heads_axis, tok_axis, query, key, value, valid_rows)

    return jax.shard_map(
        step,
        mesh=mesh,
        in_specs=placed,
        out_specs=P(("clips", "tok"), "head", None),
        check_vma=False,
    )
```

```python
import functools
import math

import jax
import jax.numpy as jnp
from jax import lax
from jax.experimental import pallas as pl
from jax.experimental.pallas import tpu as pltpu
from jax.sharding import PartitionSpec as P

HEAD_DIM = 128
TILE_H = 8
TILE_W = 8
TIME_TILES = 4
MESH = pl.DeviceIdType.MESH
GAIN = math.log2(math.e) / math.sqrt(HEAD_DIM)


def window_slots(rows_grid):
    sides = (-1, 0, 1) if rows_grid > 1 else (0,)
    around = [(down, side) for down in (-1, 0, 1) for side in sides if (down, side) != (0, 0)]
    return [(0, 0)] + around


def kernel(
    heads_axis, rows_grid,
    q_hbm, k_hbm, v_hbm, count_hbm, out_hbm,
    q_buf, k_buf, v_buf, bias_buf, s_buf, p_buf, inv_buf, acc_buf, o_buf, rows_buf, count_buf,
    local_sem, qx_send, qx_recv, kx_send, kx_recv, vx_send, vx_recv,
    bz_send, bz_recv, kz_send, kz_recv, vz_send, vz_recv, ox_send, ox_recv,
):
    slots = window_slots(rows_grid)
    width, part = q_hbm.shape[0], q_hbm.shape[1]
    tile_len, feats = q_buf.shape[1], q_buf.shape[2]
    local = feats // HEAD_DIM
    me = lax.axis_index("head")
    tok = lax.axis_index("tok")
    time, height = tok // rows_grid, tok % rows_grid
    steps = range(1, heads_axis)
    far_first = list(reversed(steps))

    def exists(j):
        down, side = slots[j]
        ok = (time + down >= 0) & (time + down < TIME_TILES)
        if side != 0:
            ok = ok & (height + side >= 0) & (height + side < rows_grid)
        return ok

    def around(j):
        return tok + slots[j][0] * rows_grid + slots[j][1]

    def opposite(j):
        return slots.index((-slots[j][0], -slots[j][1]))

    def peer(s):
        return me ^ s

    def rows(g):
        return pl.ds(pl.multiple_of(g * part, part), part)

    def cols(g):
        return pl.ds(pl.multiple_of(g * feats, feats), feats)

    def head_cols(h):
        return pl.ds(pl.multiple_of(h * HEAD_DIM, HEAD_DIM), HEAD_DIM)

    def global_cols(g, h):
        return pl.ds(pl.multiple_of((g * local + h) * HEAD_DIM, HEAD_DIM), HEAD_DIM)

    def remote(src, dst, send, recv, device):
        return pltpu.make_async_remote_copy(
            src_ref=src, dst_ref=dst, send_sem=send, recv_sem=recv,
            device_id=device, device_id_type=MESH,
        )

    def qx(s, owner):
        return remote(q_hbm.at[:, :, cols(peer(s))], q_buf.at[:, rows(owner), :],
                      qx_send.at[s], qx_recv.at[s], {"head": peer(s)})

    def kx(s, owner):
        return remote(k_hbm.at[:, :, cols(peer(s))], k_buf.at[0, :, rows(owner), :],
                      kx_send.at[s], kx_recv.at[s], {"head": peer(s)})

    def vx(h, n, s, owner):
        return remote(v_hbm.at[n, :, global_cols(peer(s), h)],
                      v_buf.at[0, n, rows(owner), head_cols(h)],
                      vx_send.at[h, n, s], vx_recv.at[h, n, s], {"head": peer(s)})

    def kz(j, s, slot):
        src = k_hbm.at[:, :, cols(me)] if s == 0 else k_buf.at[0, :, rows(peer(s)), :]
        return remote(src, k_buf.at[slot, :, rows(peer(s)), :],
                      kz_send.at[j, s], kz_recv.at[slot, s], {"tok": around(j)})

    def vz(j, h, n, s, slot):
        src = v_hbm.at[n, :, global_cols(me, h)] if s == 0 else v_buf.at[0, n, rows(peer(s)), head_cols(h)]
        return remote(src, v_buf.at[slot, n, rows(peer(s)), head_cols(h)],
                      vz_send.at[j, h, n, s], vz_recv.at[slot, h, n, s], {"tok": around(j)})

    def bz(j, slot):
        return remote(rows_buf.at[0], rows_buf.at[slot], bz_send.at[j], bz_recv.at[slot], {"tok": around(j)})

    def ox(h, c, s, owner):
        return remote(o_buf.at[c, rows(peer(s)), head_cols(h)],
                      out_hbm.at[c, :, global_cols(owner, h)],
                      ox_send.at[h, c, s], ox_recv.at[h, c, s], {"head": peer(s)})

    def each_neighbour(act):
        for j in range(1, len(slots)):
            pl.when(exists(j))(functools.partial(act, j))

    local_q = pltpu.make_async_copy(q_hbm.at[:, :, cols(me)], q_buf.at[:, rows(me), :], local_sem.at[0])
    local_k = pltpu.make_async_copy(k_hbm.at[:, :, cols(me)], k_buf.at[0, :, rows(me), :], local_sem.at[1])
    local_v = pltpu.make_async_copy(v_hbm.at[:, :, cols(me)], v_buf.at[0, :, rows(me), :], local_sem.at[2])
    local_c = pltpu.make_async_copy(count_hbm, count_buf, local_sem.at[3])

    barrier = pltpu.get_barrier_semaphore()
    for s in steps:
        pl.semaphore_signal(barrier, inc=1, device_id={"head": peer(s)}, device_id_type=MESH)
    partners = heads_axis - 1

    def greet(j):
        pl.semaphore_signal(barrier, inc=1, device_id={"tok": around(j)}, device_id_type=MESH)

    each_neighbour(greet)
    for j in range(1, len(slots)):
        partners = partners + jnp.where(exists(j), 1, 0)
    for copy in (local_c, local_q, local_k, local_v):
        copy.start()
    pl.semaphore_wait(barrier, partners)

    for s in far_first:
        kx(s, me).start()
    each_neighbour(lambda j: kz(j, 0, opposite(j)).start())
    for s in far_first:
        qx(s, me).start()
    for h in range(local):
        for n in range(width):
            for s in far_first:
                vx(h, n, s, me).start()

    local_c.wait()
    line = lax.broadcasted_iota(jnp.int32, rows_buf.shape[1:], 0)
    counts = jnp.zeros(rows_buf.shape[1:], jnp.int32)
    for n in range(width):
        counts = jnp.where(line == n, count_buf[n], counts)
    rows_buf[0] = counts

    for j in range(1, len(slots)):
        @pl.when(jnp.logical_not(exists(j)))
        def _(j=j):
            k_buf[j] = jnp.zeros(k_buf.shape[1:], k_buf.dtype)
            v_buf[j] = jnp.zeros(v_buf.shape[1:], v_buf.dtype)
            rows_buf[j] = jnp.zeros(rows_buf.shape[1:], rows_buf.dtype)

    order = [1] + [s for s in far_first if s != 1] if heads_axis > 1 else []
    for s in order:
        kx(s, peer(s)).wait_recv()
        each_neighbour(lambda j, s=s: kz(j, s, opposite(j)).start())
    near = [s for s in steps if s == 1]
    later = [s for s in order if s != 1]
    each_neighbour(lambda j: bz(j, opposite(j)).start())

    def values_on(h, n, s):
        if s != 0:
            vx(h, n, s, peer(s)).wait_recv()
        each_neighbour(lambda j: vz(j, h, n, s, opposite(j)).start())

    for h in range(local):
        for n in range(width):
            for s in [0] + near:
                values_on(h, n, s)

    for copy in (local_q, local_k, local_v):
        copy.wait()
    for s in steps:
        qx(s, peer(s)).wait_recv()

    def keys_in(j):
        bz(j, j).wait_recv()
        for s in range(heads_axis):
            kz(j, s, j).wait_recv()

    each_neighbour(keys_in)

    row = lax.broadcasted_iota(jnp.int32, bias_buf.shape[2:], 1) // TILE_W % TILE_H
    for j in range(len(slots)):
        for n in range(width):
            real = jnp.broadcast_to(rows_buf[j, n:n + 1, 0:1], row.shape)
            bias_buf[j, n] = jnp.where(row < real, 0.0, -jnp.inf)

    def window(c):
        return [(j, n) for j in range(len(slots)) for n in range(width) if abs(n - c) <= 1]

    def weigh(h, carry):
        for c in range(width):
            scratch = s_buf.at[c % s_buf.shape[0]]
            q = q_buf[c, :, head_cols(h)]
            top = None
            for i, (j, n) in enumerate(window(c)):
                s = lax.dot_general(q, k_buf[j, n, :, head_cols(h)], (((1,), (1,)), ((), ())),
                                    preferred_element_type=jnp.float32)
                s = s + bias_buf[j, n, 0:1, :]
                scratch[:, i * tile_len:(i + 1) * tile_len] = s
                for half in range(0, tile_len, 128):
                    piece = s[:, half:half + 128]
                    top = piece if top is None else jnp.maximum(top, piece)
            largest = jnp.max(top, axis=-1, keepdims=True)
            total = None
            for i in range(len(window(c))):
                for half in range(0, tile_len, 128):
                    at = slice(i * tile_len + half, i * tile_len + half + 128)
                    weight = jnp.exp2((scratch[:, at] - largest) * GAIN)
                    total = weight if total is None else total + weight
                    p_buf[h, c, :, at] = weight.astype(jnp.bfloat16)
            inverse = 1.0 / jnp.sum(total, axis=-1, keepdims=True)
            inv_buf[h, c] = jnp.broadcast_to(inverse, (tile_len, HEAD_DIM))
        for n in range(width):
            for s in later:
                values_on(h, n, s)
        return carry

    lax.fori_loop(0, local, weigh, 0)

    def local_out(h, c):
        return pltpu.make_async_copy(o_buf.at[c, rows(me), head_cols(h)],
                                     out_hbm.at[c, :, global_cols(me, h)], local_sem.at[4 + h * width + c])

    if heads_axis % 2 == 0:
        half = heads_axis // 2
        span = tile_len // 2
        side = me // half
        blocks = [
            (pl.ds(pl.multiple_of((1 - side) * span, span), span), [s for s in far_first if s >= half]),
            (pl.ds(pl.multiple_of(side * span, span), span), [s for s in far_first if s < half]),
        ]
    else:
        blocks = [(slice(None), far_first)]

    def mix(h, carry):
        def gather(c, at, picked):
            summed = None
            for i, (j, n) in enumerate(window(c)):
                if picked(j, n):
                    term = jnp.dot(p_buf[h, c, at, i * tile_len:(i + 1) * tile_len],
                                   v_buf[j, n, :, head_cols(h)], preferred_element_type=jnp.float32)
                    summed = term if summed is None else summed + term
            return summed

        for c in range(width):
            acc_buf[c] = gather(c, slice(None), lambda j, n: j == 0)
        for n in range(width):
            def values_in(j, n=n):
                for s in range(heads_axis):
                    vz(j, h, n, s, j).wait_recv()

            each_neighbour(values_in)
            here = [c for c in range(width) if abs(n - c) <= 1]
            done = [c for c in here if n == min(c + 1, width - 1)]
            for at, partners_at in blocks:
                for c in done:
                    summed = acc_buf[c, at] + gather(c, at, lambda j, m: j != 0 and m == n)
                    o_buf[c, at, head_cols(h)] = (summed * inv_buf[h, c, at]).astype(o_buf.dtype)
                    for s in partners_at:
                        ox(h, c, s, me).start()
            for c in done:
                local_out(h, c).start()
            for c in here:
                if c not in done:
                    acc_buf[c] = acc_buf[c] + gather(c, slice(None), lambda j, m: j != 0 and m == n)
        return carry

    lax.fori_loop(0, local, mix, 0)

    for s in steps:
        kx(s, me).wait_send()
        qx(s, me).wait_send()
        for h in range(local):
            for n in range(width):
                vx(h, n, s, me).wait_send()

    def sent(j):
        bz(j, opposite(j)).wait_send()
        for s in range(heads_axis):
            kz(j, s, opposite(j)).wait_send()
            for h in range(local):
                for n in range(width):
                    vz(j, h, n, s, opposite(j)).wait_send()

    each_neighbour(sent)
    for h in range(local):
        for c in range(width):
            local_out(h, c).wait()
            for s in steps:
                ox(h, c, s, me).wait_send()
                ox(h, c, s, peer(s)).wait_recv()


def body(heads_axis, tok_axis, query, key, value, valid_rows):
    width, part, wide = query.shape
    rows_grid = tok_axis // TIME_TILES
    tile_len, feats = part * heads_axis, wide // heads_axis
    local = feats // HEAD_DIM
    slots = len(window_slots(rows_grid))
    most = slots * min(width, 3) * tile_len
    dma = pltpu.SemaphoreType.DMA
    any_space = pl.BlockSpec(memory_space=pl.ANY)
    return pl.pallas_call(
        functools.partial(kernel, heads_axis, rows_grid),
        out_shape=jax.ShapeDtypeStruct(query.shape, query.dtype),
        in_specs=[pl.BlockSpec(memory_space=pltpu.HBM)] * 4,
        out_specs=any_space,
        scratch_shapes=[
            pltpu.VMEM((width, tile_len, feats), jnp.bfloat16),
            pltpu.VMEM((slots, width, tile_len, feats), jnp.bfloat16),
            pltpu.VMEM((slots, width, tile_len, feats), jnp.bfloat16),
            pltpu.VMEM((slots, width, 8, tile_len), jnp.float32),
            pltpu.VMEM((3 if slots <= 3 else 1, tile_len, most), jnp.float32),
            pltpu.VMEM((local, width, tile_len, most), jnp.bfloat16),
            pltpu.VMEM((local, width, tile_len, HEAD_DIM), jnp.float32),
            pltpu.VMEM((width, tile_len, HEAD_DIM), jnp.float32),
            pltpu.VMEM((width, tile_len, feats), jnp.bfloat16),
            pltpu.VMEM((slots, -(-width // 8) * 8, 128), jnp.int32),
            pltpu.SMEM((width,), jnp.int32),
            dma((4 + local * width,)),
            dma((heads_axis,)), dma((heads_axis,)),
            dma((heads_axis,)), dma((heads_axis,)),
            dma((local, width, heads_axis)), dma((local, width, heads_axis)),
            dma((slots,)), dma((slots,)),
            dma((slots, heads_axis)), dma((slots, heads_axis)),
            dma((slots, local, width, heads_axis)), dma((slots, local, width, heads_axis)),
            dma((local, width, heads_axis)), dma((local, width, heads_axis)),
        ],
        compiler_params=pltpu.CompilerParams(
            collective_id=0, has_side_effects=True, vmem_limit_bytes=36_000_000 if slots <= 3 else 63_000_000
        ),
    )(*(pltpu.with_memory_space_constraint(x, pltpu.HBM) for x in (query, key, value, valid_rows)))


def by_head(
    q_hbm, k_hbm, v_hbm, count_hbm, out_hbm,
    q_buf, k_buf, v_buf, bias_buf, s_buf, p_buf, inv_buf, acc_buf, o_buf, rows_buf, count_buf,
    lq_sem, lk_sem, lv_sem, lc_sem, lo_sem, qx_send, qx_recv, kx_send, kx_recv, vx_send, vx_recv,
    bz_send, bz_recv, kz_send, kz_recv, vz_send, vz_recv, ox_send, ox_recv,
):
    local, width, tile_len = q_buf.shape[0], q_buf.shape[1], q_buf.shape[2]
    part = q_hbm.shape[1]
    me = lax.axis_index("head")
    tok = lax.axis_index("tok")
    side = me // 2
    half = tile_len // 2
    far, last = (3, 2), local - 1
    slots = (0, -1, 1)
    opposite = (0, 2, 1)

    def exists(j):
        return (tok + slots[j] >= 0) & (tok + slots[j] < TIME_TILES)

    def peer(s):
        return me ^ s

    def rows(g):
        return pl.ds(pl.multiple_of(g * part, part), part)

    def cols(g, h):
        return pl.ds(pl.multiple_of((g * local + h) * HEAD_DIM, HEAD_DIM), HEAD_DIM)

    def remote(src, dst, send, recv, device):
        return pltpu.make_async_remote_copy(
            src_ref=src, dst_ref=dst, send_sem=send, recv_sem=recv,
            device_id=device, device_id_type=MESH,
        )

    def spread(hbm, buf, send, recv):
        def copy(h, s, owner):
            return remote(hbm.at[:, :, cols(peer(s), h)], buf(h).at[:, rows(owner), :],
                          send.at[h, s - 1], recv.at[h, s - 1], {"head": peer(s)})
        return copy

    qx = spread(q_hbm, lambda h: q_buf.at[h], qx_send, qx_recv)
    kx = spread(k_hbm, lambda h: k_buf.at[0, h], kx_send, kx_recv)
    vx = spread(v_hbm, lambda h: v_buf.at[0, h], vx_send, vx_recv)

    def along(hbm, buf, send, recv):
        def copy(j, h, s, slot, n=None):
            pick = slice(None) if n is None else slice(n, n + 1)
            at = h * 4 + s if not n else local * 4 + (s - 2) * (width - 1) + n - 1
            src = hbm.at[pick, :, cols(me, h)] if s == 0 else buf.at[0, h, pick, rows(peer(s)), :]
            return remote(src, buf.at[slot, h, pick, rows(peer(s)), :],
                          send.at[j - 1, at], recv.at[slot - 1, at], {"tok": tok + slots[j]})
        return copy

    kz = along(k_hbm, k_buf, kz_send, kz_recv)
    vz = along(v_hbm, v_buf, vz_send, vz_recv)

    def vz_tiles(h, s):
        return tuple(range(width)) if h == last and s in far else (None,)

    def bz(j, slot):
        return remote(rows_buf.at[0], rows_buf.at[slot], bz_send.at[j - 1], bz_recv.at[slot - 1], {"tok": tok + slots[j]})

    def ox(h, c, s, owner):
        return remote(o_buf.at[h, c, rows(peer(s)), :], out_hbm.at[c, :, cols(owner, h)],
                      ox_send.at[h, c, s - 1], ox_recv.at[h, c, s - 1], {"head": peer(s)})

    def own(hbm, buf, sem):
        return [pltpu.make_async_copy(hbm.at[:, :, cols(me, h)], buf(h).at[:, rows(me), :], sem.at[h])
                for h in range(local)]

    own_k = own(k_hbm, lambda h: k_buf.at[0, h], lk_sem)
    own_v = own(v_hbm, lambda h: v_buf.at[0, h], lv_sem)
    own_q = own(q_hbm, lambda h: q_buf.at[h], lq_sem)
    own_c = pltpu.make_async_copy(count_hbm, count_buf, lc_sem)

    def own_o(h, c):
        return pltpu.make_async_copy(o_buf.at[h, c, rows(me), :], out_hbm.at[c, :, cols(me, h)], lo_sem.at[h, c])

    def each_neighbour(act):
        for j in (1, 2):
            pl.when(exists(j))(functools.partial(act, j))

    barrier = pltpu.get_barrier_semaphore()

    def greet(j):
        pl.semaphore_signal(barrier, inc=1, device_id={"tok": tok + slots[j]}, device_id_type=MESH)

    each_neighbour(greet)
    for s in (2, 3, 1):
        pl.semaphore_signal(barrier, inc=1, device_id={"head": peer(s)}, device_id_type=MESH)
    own_c.start()
    for h in range(local):
        own_k[h].start()
        own_v[h].start()
    for h in range(local):
        own_q[h].start()
    pl.semaphore_wait(barrier, 3 + jnp.where(exists(1), 1, 0) + jnp.where(exists(2), 1, 0))

    def across(copy, h):
        for s in far:
            copy(h, s, me).start()

    def beside(copy, h):
        copy(h, 1, me).start()

    def onward(copy, h, s, tiles=(None,)):
        def act(j):
            for n in tiles:
                copy(j, h, s, opposite[j], n).start()
        each_neighbour(act)

    def onward_v(h, s):
        onward(vz, h, s, vz_tiles(h, s))

    across(kx, 0)
    onward(kz, 0, 0)
    beside(kx, 0)
    across(vx, 0)
    onward_v(0, 0)
    beside(vx, 0)
    across(qx, 0)
    for h in range(1, local):
        beside(kx, h)
        beside(vx, h)
    across(kx, 1)
    onward(kz, 1, 0)
    across(vx, 1)
    onward_v(1, 0)
    across(kx, 2)
    across(qx, 1)
    across(vx, 2)
    across(qx, 2)
    for h in range(local):
        beside(qx, h)

    for h in (0, 1):
        kx(h, 1, peer(1)).wait_recv()
        onward(kz, h, 1)
        vx(h, 1, peer(1)).wait_recv()
        onward_v(h, 1)
    for j in (1, 2):
        @pl.when(jnp.logical_not(exists(j)))
        def _(j=j):
            k_buf[j] = jnp.zeros(k_buf.shape[1:], k_buf.dtype)
            v_buf[j] = jnp.zeros(v_buf.shape[1:], v_buf.dtype)
            rows_buf[j] = jnp.zeros(rows_buf.shape[1:], rows_buf.dtype)
    own_c.wait()
    line = lax.broadcasted_iota(jnp.int32, rows_buf.shape[1:], 0)
    counts = jnp.zeros(rows_buf.shape[1:], jnp.int32)
    for n in range(width):
        counts = jnp.where(line == n, count_buf[n], counts)
    rows_buf[0] = counts
    each_neighbour(lambda j: bz(j, opposite[j]).start())
    for h in range(local):
        own_k[h].wait()
        own_v[h].wait()
    for s in far:
        kx(0, s, peer(s)).wait_recv()
        onward(kz, 0, s)
    for s in far:
        vx(0, s, peer(s)).wait_recv()
        onward_v(0, s)
    onward(kz, last, 0)
    kx(last, 1, peer(1)).wait_recv()
    onward(kz, last, 1)
    vx(last, 1, peer(1)).wait_recv()

    each_neighbour(lambda j: bz(j, j).wait_recv())
    row = lax.broadcasted_iota(jnp.int32, bias_buf.shape[2:], 1) // TILE_W % TILE_H
    for j in range(3):
        for n in range(width):
            real = jnp.broadcast_to(rows_buf[j, n:n + 1, 0:1], row.shape)
            bias_buf[j, n] = jnp.where(row < real, 0.0, -jnp.inf)

    for s in far:
        kx(1, s, peer(s)).wait_recv()
        onward(kz, 1, s)
    for s in far:
        vx(1, s, peer(s)).wait_recv()
        onward_v(1, s)

    def window(c):
        return [(j, n) for j in range(3) for n in range(width) if abs(n - c) <= 1]

    def queries_in(h):
        own_q[h].wait()
        for s in (1, 2, 3):
            qx(h, s, peer(s)).wait_recv()

    def keys_in(h):
        def act(j):
            for s in range(4):
                kz(j, h, s, j).wait_recv()
        each_neighbour(act)

    def values_in(h, which, tiles=None):
        def act(j):
            for s in which:
                for n in (tiles if tiles is not None else vz_tiles(h, s)):
                    vz(j, h, s, j, n).wait_recv()
        each_neighbour(act)

    def weigh(h):
        for c in range(width):
            scratch = s_buf.at[c]
            q = q_buf[h, c]
            top = None
            for i, (j, n) in enumerate(window(c)):
                s = lax.dot_general(q, k_buf[j, h, n], (((1,), (1,)), ((), ())),
                                    preferred_element_type=jnp.float32)
                s = s + bias_buf[j, n, 0:1, :]
                scratch[:, i * tile_len:(i + 1) * tile_len] = s
                for at in range(0, tile_len, 128):
                    piece = s[:, at:at + 128]
                    top = piece if top is None else jnp.maximum(top, piece)
            largest = jnp.max(top, axis=-1, keepdims=True)
            total = None
            for i in range(len(window(c))):
                for at in range(0, tile_len, 128):
                    at = slice(i * tile_len + at, i * tile_len + at + 128)
                    weight = jnp.exp2((scratch[:, at] - largest) * GAIN)
                    total = weight if total is None else total + weight
                    p_buf[c, :, at] = weight.astype(jnp.bfloat16)
            inverse = 1.0 / jnp.sum(total, axis=-1, keepdims=True)
            inv_buf[c] = jnp.broadcast_to(inverse, (tile_len, HEAD_DIM))

    there = pl.ds(pl.multiple_of((1 - side) * half, half), half)
    here = pl.ds(pl.multiple_of(side * half, half), half)
    blocks = ((there, far), (here, (1,)))

    def mixed(h, c, at, picked, keys=None):
        summed = None
        for i, (j, n) in enumerate(window(c)):
            if picked(j, n):
                if keys is None:
                    p, v = p_buf[c, at, i * tile_len:(i + 1) * tile_len], v_buf[j, h, n]
                else:
                    span = pl.ds(pl.multiple_of(i * tile_len + keys * half, half), half)
                    p, v = p_buf[c, at, span], v_buf[j, h, n, pl.ds(pl.multiple_of(keys * half, half), half), :]
                term = jnp.dot(p, v, preferred_element_type=jnp.float32)
                summed = term if summed is None else summed + term
        return summed

    def leave(h, c, at, partners, summed):
        o_buf[h, c, at, :] = (summed * inv_buf[c, at]).astype(o_buf.dtype)
        for s in partners:
            ox(h, c, s, me).start()

    def mix(h):
        for c in range(width):
            for at, partners in blocks:
                leave(h, c, at, partners, mixed(h, c, at, lambda j, n: True))
            own_o(h, c).start()

    def mix_last(h):
        for c in range(width):
            acc_buf[c] = mixed(h, c, slice(None), lambda j, n: j == 0)
        values_in(h, (0, 1))
        for c in range(width):
            acc_buf[c] = acc_buf[c] + mixed(h, c, slice(None), lambda j, n: j != 0, side)
        for n in range(width):
            values_in(h, far, (n,))
            near = [c for c in range(width) if abs(n - c) <= 1]
            done = [c for c in near if n == min(c + 1, width - 1)]
            for at, partners in blocks:
                for c in done:
                    leave(h, c, at, partners,
                          acc_buf[c, at] + mixed(h, c, at, lambda j, m: j != 0 and m == n, 1 - side))
            for c in done:
                own_o(h, c).start()
            for c in near:
                if c not in done:
                    acc_buf[c] = acc_buf[c] + mixed(h, c, slice(None), lambda j, m: j != 0 and m == n, 1 - side)

    queries_in(0)
    keys_in(0)
    weigh(0)
    for s in far:
        kx(last, s, peer(s)).wait_recv()
        onward(kz, last, s)
    onward_v(last, 0)
    onward_v(last, 1)
    values_in(0, range(4))
    mix(0)
    for s in far:
        vx(last, s, peer(s)).wait_recv()
    for n in range(width):
        for s in far:
            onward(vz, last, s, (n,))
    queries_in(1)
    keys_in(1)
    weigh(1)
    values_in(1, range(4))
    mix(1)
    queries_in(last)
    keys_in(last)
    weigh(last)
    mix_last(last)

    for h in range(local):
        for s in (1, 2, 3):
            kx(h, s, me).wait_send()
            vx(h, s, me).wait_send()
            qx(h, s, me).wait_send()

    def sent(j):
        bz(j, opposite[j]).wait_send()
        for h in range(local):
            for s in range(4):
                kz(j, h, s, opposite[j]).wait_send()
                for n in vz_tiles(h, s):
                    vz(j, h, s, opposite[j], n).wait_send()

    each_neighbour(sent)
    for h in range(local):
        for c in range(width):
            own_o(h, c).wait()
            for s in (1, 2, 3):
                ox(h, c, s, me).wait_send()
                ox(h, c, s, peer(s)).wait_recv()


def body_by_head(query, key, value, valid_rows):
    width, part, wide = query.shape
    tile_len, local = part * 4, wide // 4 // HEAD_DIM
    most = 3 * min(width, 3) * tile_len
    dma = pltpu.SemaphoreType.DMA
    return pl.pallas_call(
        by_head,
        out_shape=jax.ShapeDtypeStruct(query.shape, query.dtype),
        in_specs=[pl.BlockSpec(memory_space=pltpu.HBM)] * 4,
        out_specs=pl.BlockSpec(memory_space=pl.ANY),
        scratch_shapes=[
            pltpu.VMEM((local, width, tile_len, HEAD_DIM), jnp.bfloat16),
            pltpu.VMEM((3, local, width, tile_len, HEAD_DIM), jnp.bfloat16),
            pltpu.VMEM((3, local, width, tile_len, HEAD_DIM), jnp.bfloat16),
            pltpu.VMEM((3, width, 8, tile_len), jnp.float32),
            pltpu.VMEM((width, tile_len, most), jnp.float32),
            pltpu.VMEM((width, tile_len, most), jnp.bfloat16),
            pltpu.VMEM((width, tile_len, HEAD_DIM), jnp.float32),
            pltpu.VMEM((width, tile_len, HEAD_DIM), jnp.float32),
            pltpu.VMEM((local, width, tile_len, HEAD_DIM), jnp.bfloat16),
            pltpu.VMEM((3, -(-width // 8) * 8, 128), jnp.int32),
            pltpu.SMEM((width,), jnp.int32),
            dma((local,)), dma((local,)), dma((local,)), dma(()), dma((local, width)),
            dma((local, 3)), dma((local, 3)), dma((local, 3)), dma((local, 3)), dma((local, 3)), dma((local, 3)),
            dma((2,)), dma((2,)),
            dma((2, local * 4)), dma((2, local * 4)),
            dma((2, local * 4 + 2 * (width - 1))), dma((2, local * 4 + 2 * (width - 1))),
            dma((local, width, 3)), dma((local, width, 3)),
        ],
        compiler_params=pltpu.CompilerParams(
            collective_id=0, has_side_effects=True, vmem_limit_bytes=36_000_000
        ),
    )(*(pltpu.with_memory_space_constraint(x, pltpu.HBM) for x in (query, key, value, valid_rows)))


def solution(mesh):
    placed = (
        P(("clips", "tok"), "head", None),
        P(("clips", "tok"), "head", None),
        P(("clips", "tok"), "head", None),
        P(("clips", "tok")),
    )
    heads_axis, tok_axis = mesh.shape["head"], mesh.shape["tok"]

    def step(query, key, value, valid_rows):
        if heads_axis == 4 and tok_axis == TIME_TILES and query.shape[2] == 4 * 3 * HEAD_DIM:
            return body_by_head(query, key, value, valid_rows)
        return body(heads_axis, tok_axis, query, key, value, valid_rows)

    return jax.shard_map(
        step,
        mesh=mesh,
        in_specs=placed,
        out_specs=P(("clips", "tok"), "head", None),
        check_vma=False,
    )
```
